256 devices in a mesh: dp: 16 (over z, core), tm: 16 (over x, y).
Axes of the slice: x: 4, y: 4, z: 8, core: 2. Of those that a mesh axis runs over, the one named last changes fastest.
Arguments:
- video_tokens: bfloat16 [16, 128, 196, 768], P('dp', 'tm'), may hold values from -6 to 6
- norm_gain: bfloat16 [768], P('dp'), may hold values from 0.25 to 1.75
- norm_bias: bfloat16 [768], P('dp'), may hold values from -3 to 3
- qkv_weight: bfloat16 [768, 1152], P('dp'), may hold values from -16 to 16
- frame_counts: int32 [16], P('dp'), may hold values from 16 to 128, as said below
- clip_starts: int32 [16, 8], P('dp'), may hold values 0 or 1
- frame_kept: int32 [16, 128], P('dp'), may hold values 0 or 1
- attended_grad: bfloat16 [16, 128, 196, 384], P('dp', 'tm'), may hold values from -6 to 6
Outputs:
- attended: bfloat16 [16, 128, 196, 384], P('dp', 'tm')
- tokens_grad: bfloat16 [16, 128, 196, 768], P('dp', 'tm')
- qkv_weight_grad: float32 [768, 1152], P('dp')
- gain_grad: float32 [768], P('dp')
- bias_grad: float32 [768], P('dp')
The draws below stay inside these ranges and needn't reach their ends.
Inputs may be any that keep to these rules, and one draw needn't show every extreme that they name: `frame_counts`: every count is a multiple of 16; some video has 128 frames and some video has 16.
All inputs are finite; a program needn't handle non-finite values. No bound on the sum of `clip_starts` or of `frame_kept` on one device may be relied on, other than what follows from the above.
Results may differ from the reference program's by a relative error of at most 0.02.
Values may be sent and summed in bfloat16 or wider, within the bound.
A program may use at most 128 MiB of HBM per device.

```python
import jax
import jax.numpy as jnp
from jax import lax

D = 768
HEADS = 6
PATCHES = 196
BLOCK = 16
HD = 384
FRAMES = 128
NB = 8
VIDEOS = 16


def draw_qkv_weight(key, part):
    normal_part = jax.random.normal(jax.random.fold_in(key, 11), (D, 3 * HD), jnp.float32) * D ** (-0.5)
    return jnp.clip(normal_part, -16.0, 16.0).astype(jnp.bfloat16)


def draw_frame_counts(key, part):
    blocks = jax.random.randint(jax.random.fold_in(key, 21), (VIDEOS,), 1, NB + 1)
    order = jax.random.permutation(jax.random.fold_in(key, 22), VIDEOS)
    blocks = blocks.at[order[0]].set(NB)
    blocks = blocks.at[order[1]].set(1)
    return (blocks * BLOCK).astype(jnp.int32)


def place_ends(values, stream_key, least, largest):
    extent = values.shape
    spot = [jax.random.randint(jax.random.fold_in(stream_key, axis), (), 0, extent[axis]) for axis in range(len(extent))]
    values = values.at[tuple(spot)].set(least)
    longest = extent.index(max(extent))
    spot[longest] = (spot[longest] + 1) % extent[longest]
    return values.at[tuple(spot)].set(largest)


def strengthened(array, rng, source, target, blocks, factor):
    owner, partner = [(jnp.arange(array.shape[position]) // (array.shape[position] // blocks)).reshape([-1 if axis == position else 1 for axis in range(array.ndim)]) for position in (source, target)]
    chosen = jax.random.permutation(rng, blocks)[partner]
    strong = (owner == chosen) | (owner == (partner + blocks // 2) % blocks)
    return jnp.where(strong, factor * array, array)


def level_of(key, extent, cuts, low, high):
    loudness = 1.0
    for dim, blocks in cuts:
        heights = jax.random.uniform(jax.random.fold_in(jax.random.fold_in(key, 6), dim), (blocks,), jnp.float32, low / len(cuts), high / len(cuts))
        loudness = loudness * jnp.repeat(jnp.exp(heights), extent[dim] // blocks).reshape((-1,) + (1,) * (len(extent) - 1 - dim))
    return loudness


def gaussian(stream_key, shape, scale, reach, split=(), kind=jnp.bfloat16):
    drawn = jax.random.normal(stream_key, shape, jnp.float32) * scale
    if len(split) > 0:
        drawn = level_of(stream_key, shape, split, -0.22, 0.18) * drawn
    return jnp.clip(drawn, min=-reach, max=reach).astype(kind)


def heavy_noise(stream_key, dims, scale, reach, pieces, heavy, kind=jnp.bfloat16):
    array = scale * jax.random.normal(stream_key, dims, jnp.float32)
    if pieces:
        array = array * level_of(stream_key, dims, pieces, -0.22, 0.18)
    return jnp.clip(strengthened(array, jax.random.fold_in(stream_key, 3), *heavy), -reach, reach).astype(kind)


def setup_inputs(seed: int = 0) -> dict:
    splits = jax.random.split(jax.random.key(seed), 9)
    video_tokens = heavy_noise(splits[0], (VIDEOS, FRAMES, PATCHES, D), 1.0, 6.0, ((0, 16), (1, 16)), (0, 3, 16, 2.0))
    norm_gain = jnp.clip(1.0 + 0.15 * jax.random.normal(splits[1], (D,), jnp.float32), 0.25, 1.75).astype(jnp.bfloat16)
    norm_bias = gaussian(splits[2], (D,), 0.5, 3.0, ((0, 16),))
    qkv_weight = draw_qkv_weight(jax.random.fold_in(splits[8], 71), 0)
    frame_counts = draw_frame_counts(jax.random.fold_in(splits[8], 71), 0)
    clip_starts = place_ends((jax.random.randint(splits[5], (VIDEOS, NB), 0, 3) < 1).astype(jnp.int32), jax.random.fold_in(splits[5], 1), 0, 1)
    frame_kept = place_ends((jax.random.randint(splits[6], (VIDEOS, FRAMES), 0, 8) < 7).astype(jnp.int32), jax.random.fold_in(splits[6], 1), 0, 1)
    attended_grad = gaussian(splits[7], (VIDEOS, FRAMES, PATCHES, HD), 1.0, 6.0, ((0, 16), (1, 16)))
    return dict(video_tokens=video_tokens, norm_gain=norm_gain, norm_bias=norm_bias, qkv_weight=qkv_weight, frame_counts=frame_counts, clip_starts=clip_starts, frame_kept=frame_kept, attended_grad=attended_grad)


masked_value = -1e+30
epsilon = 1e-05

def standardize(rows):
    centred = rows - lax.optimization_barrier(jnp.mean(rows, axis=-1, keepdims=True))
    inverse = lax.rsqrt(lax.optimization_barrier(jnp.mean(centred * centred, axis=-1, keepdims=True)) + epsilon)
    return (centred * inverse, inverse)

def frame_masks(frame_count, starts, kept, frames):
    frame_index = jnp.arange(frames, dtype=jnp.int32)
    block_index = jnp.arange(starts.shape[0], dtype=jnp.int32)
    flags = jnp.where(block_index > 0, starts, 0)
    clip_of_block = jnp.cumsum(flags).astype(jnp.int32)
    clip_number = clip_of_block[(frame_index // BLOCK).astype(jnp.int32)]
    usable = (frame_index < frame_count) & (kept == 1)
    same_clip = clip_number[:, None] == clip_number[None, :]
    allowed = same_clip & (usable[None, :] | (frame_index[:, None] == frame_index[None, :]))
    return (allowed, frame_index < frame_count)

def split_heads(projected, start, joined):
    return projected[:, :, start:start + joined].reshape(projected.shape[0], projected.shape[1], HEADS, joined // HEADS).astype(jnp.float32)

def attend(projected, allowed, valid):
    frames, patch_rows = (projected.shape[0], projected.shape[1])
    joined = projected.shape[2] // 3
    scale = (joined // HEADS) ** (-0.5)
    queries = split_heads(projected, 0, joined)
    key_rows = split_heads(projected, joined, joined)
    values = split_heads(projected, 2 * joined, joined)
    scores = jnp.einsum('fphd,gphd->phfg', queries, key_rows) * scale
    scores = jnp.where(allowed, scores, masked_value)
    shifted = jnp.exp(scores - lax.optimization_barrier(jnp.max(scores, axis=-1, keepdims=True)))
    weights = shifted / lax.optimization_barrier(jnp.sum(shifted, axis=-1, keepdims=True))
    rounded = weights.astype(jnp.bfloat16).astype(jnp.float32)
    mixed = jnp.einsum('phfg,gphd->fphd', rounded, values)
    mixed = jnp.where(valid[:, None, None, None], mixed, 0.0)
    return (mixed.reshape(frames, patch_rows, joined).astype(jnp.bfloat16), weights)

def attend_back(projected, weights, upstream, valid):
    frames, patch_rows = (projected.shape[0], projected.shape[1])
    joined = projected.shape[2] // 3
    head_width = joined // HEADS
    scale = head_width ** (-0.5)
    queries = split_heads(projected, 0, joined)
    key_rows = split_heads(projected, joined, joined)
    values = split_heads(projected, 2 * joined, joined)
    kept_grad = jnp.where(valid[:, None, None], upstream, jnp.zeros_like(upstream))
    kept_grad = kept_grad.reshape(frames, patch_rows, HEADS, head_width).astype(jnp.float32)
    rounded = weights.astype(jnp.bfloat16).astype(jnp.float32)
    weight_grad = jnp.einsum('fphd,gphd->phfg', kept_grad, values)
    value_grad = jnp.einsum('phfg,fphd->gphd', rounded, kept_grad)
    inner = lax.optimization_barrier(jnp.sum(weight_grad * weights, axis=-1, keepdims=True))
    score_grad = (weights * (weight_grad - inner) * scale).astype(jnp.bfloat16).astype(jnp.float32)
    query_grad = jnp.einsum('phfg,gphd->fphd', score_grad, key_rows)
    key_grad = jnp.einsum('phfg,fphd->gphd', score_grad, queries)
    parts = [query_grad, key_grad, value_grad]
    return jnp.concatenate([piece.reshape(frames, patch_rows, joined) for piece in parts], axis=2).astype(jnp.bfloat16)

def reference(video_tokens, norm_gain, norm_bias, qkv_weight, frame_counts, clip_starts, frame_kept, attended_grad):
    gain_wide = norm_gain.astype(jnp.float32)
    bias_wide = norm_bias.astype(jnp.float32)
    columns = qkv_weight.shape[1]

    def one_video(carry, inputs):
        tokens, frame_count, starts, kept, upstream = inputs
        frames, patches, model_width = tokens.shape
        standard, inverse = standardize(tokens.reshape(-1, model_width).astype(jnp.float32))
        normed = (standard * gain_wide + bias_wide).astype(jnp.bfloat16)
        projected = jnp.dot(normed, qkv_weight, preferred_element_type=jnp.float32).astype(jnp.bfloat16)
        projected = projected.reshape(frames, patches, columns)
        allowed, valid = frame_masks(frame_count, starts, kept, frames)
        mixed, weights = attend(projected, allowed, valid)
        projected_grad = attend_back(projected, weights, upstream, valid).reshape(-1, columns)
        weight_grad = lax.dot_general(normed, projected_grad, (((0,), (0,)), ((), ())), preferred_element_type=jnp.float32)
        normed_grad = lax.dot_general(projected_grad, qkv_weight, (((1,), (1,)), ((), ())), preferred_element_type=jnp.float32)
        normed_grad = lax.optimization_barrier(normed_grad.astype(jnp.bfloat16)).astype(jnp.float32)
        gain_part = lax.optimization_barrier(jnp.sum(normed_grad * standard, axis=0))
        bias_part = lax.optimization_barrier(jnp.sum(normed_grad, axis=0))
        scaled = normed_grad * gain_wide
        tokens_grad = inverse * (scaled - lax.optimization_barrier(jnp.mean(scaled, axis=-1, keepdims=True)) - standard * lax.optimization_barrier(jnp.mean(scaled * standard, axis=-1, keepdims=True)))
        tokens_grad = tokens_grad.astype(jnp.bfloat16).reshape(frames, patches, model_width)
        total_w, total_gain, total_bias = carry
        return ((total_w + weight_grad, total_gain + gain_part, total_bias + bias_part), (mixed, tokens_grad))
    start = (jnp.zeros(qkv_weight.shape, jnp.float32), jnp.zeros(norm_gain.shape, jnp.float32), jnp.zeros(norm_bias.shape, jnp.float32))
    sums, stacked = lax.scan(one_video, start, (video_tokens, frame_counts, clip_starts, frame_kept, attended_grad))
    return (stacked[0], stacked[1], sums[0], sums[1], sums[2])
```

```python
import functools

import jax
import jax.numpy as jnp
from jax import lax
from jax.experimental import pallas as pl
from jax.experimental.pallas import tpu as pltpu
from jax.sharding import PartitionSpec as P

F32 = jnp.float32
BF = jnp.bfloat16
MESH = pl.DeviceIdType.MESH
BLOCK = 16
FR = 128
D = 768
C = 1152
HD = 384
EPS = 1e-05
MASKED = -1e30
OFFS = [(dx, dy) for dx in range(4) for dy in range(4) if (dx, dy) != (0, 0)]
WB = 56
NN = (((1,), (0,)), ((), ()))
NT = (((1,), (1,)), ((), ()))
TN = (((0,), (0,)), ((), ()))


def dot(a, b, dims=NN):
    return lax.dot_general(a, b, dims, preferred_element_type=F32)


def wait(ref, sem):
    pltpu.make_async_copy(ref, ref, sem).wait()


def kernel(
    xt, gt, wl, mask, valid,
    ato, tgo, dwo, gbo,
    xbuf, gbuf, abuf, tbuf, wall, wfull, wt, dw, gb,
    normed, mst, rst, proj, dproj, nt, ng, gacc, bacc,
    senda, recva, sendb, recvb, totb, crx, red, fin,
    pk, pkp, pk2, pkz, pk3, pkt,
    rx, rg, sx, sg, orx, org, osx, osg,
    wsend, wrecv, psend, precv, lsem,
    asend, arecv, bsend, brecv, csend, crecv, fsend, frecv,
    k1s, k1r, k2s, k2r, k3s, k3r,
):
    dp = lax.axis_index("dp")
    me = lax.axis_index("tm")
    z, c = dp // 2, dp % 2
    x, y = me // 4, me % 4
    partner = dp + 1 - 2 * c
    tms = [lax.rem(x + dx, 4) * 4 + lax.rem(y + dy, 4) for dx, dy in OFFS]
    zs = [lax.rem(z + k, 8) for k in range(8)]
    has13 = me % 5 == 0

    def remote(src, dst, ssem, rsem, **device):
        return pltpu.make_async_remote_copy(
            src_ref=src, dst_ref=dst, send_sem=ssem, recv_sem=rsem,
            device_id=device, device_id_type=MESH,
        )

    barrier = pltpu.get_barrier_semaphore()
    for t in tms:
        pl.semaphore_signal(barrier, inc=1, device_id={"tm": t}, device_id_type=MESH)
    for k in range(1, 8):
        pl.semaphore_signal(barrier, inc=1, device_id={"dp": zs[k] * 2 + c}, device_id_type=MESH)
    pl.semaphore_signal(barrier, inc=1, device_id={"dp": partner}, device_id_type=MESH)
    pl.semaphore_wait(barrier, 23)

    own = pltpu.make_async_copy(wl, wall.at[dp], lsem)
    own.start()
    for k in (4, 3, 5, 2, 6, 1, 7):
        remote(wl, wall.at[dp], wsend, wrecv.at[k], dp=zs[k] * 2 + c).start()
    remote(wl, wall.at[dp], psend, precv, dp=partner).start()

    def send_in(p, carry):
        for t in tms:
            remote(xt.at[p * 16 + t], xbuf.at[p, me], sx, rx.at[p], tm=t).start()
            remote(gt.at[p * 16 + t], gbuf.at[p, me], sg, rg.at[p], tm=t).start()
        pltpu.make_async_copy(xt.at[p * 16 + me], xbuf.at[p, me], rx.at[p]).start()
        pltpu.make_async_copy(gt.at[p * 16 + me], gbuf.at[p, me], rg.at[p]).start()
        return carry

    lax.fori_loop(0, 12, send_in, 0)
    for i in range(4):
        @pl.when(me != 5 * i)
        def _():
            remote(xt.at[192 + i], xbuf.at[12, me], sx, rx.at[12], tm=5 * i).start()
            remote(gt.at[192 + i], gbuf.at[12, me], sg, rg.at[12], tm=5 * i).start()

        @pl.when(me == 5 * i)
        def _():
            pltpu.make_async_copy(xt.at[192 + i], xbuf.at[12, me], rx.at[12]).start()
            pltpu.make_async_copy(gt.at[192 + i], gbuf.at[12, me], rg.at[12]).start()

    xbuf[13] = jnp.zeros_like(xbuf[13])
    gbuf[13] = jnp.zeros_like(gbuf[13])
    dw[...] = jnp.zeros_like(dw)
    gacc[...] = jnp.zeros_like(gacc)
    bacc[...] = jnp.zeros_like(bacc)

    for k in (1, 7, 2, 6, 3, 5, 4):
        source = lax.rem(z + 8 - k, 8) * 2 + c
        wait(wall.at[source], wrecv.at[k])
        remote(wall.at[source], wall.at[source], psend, precv, dp=partner).start()
    own.wait()
    wait(wall.at[pl.ds(0, 8)], precv)
    for d in range(16):
        wfull[48 * d : 48 * (d + 1), :] = wall[d, 0:48, :]
    gb[...] = jnp.sum(wall[:, 48:56, 0:D].astype(F32), axis=0)
    for j in range(9):
        wt[128 * j : 128 * (j + 1), :] = wfull[:, 128 * j : 128 * (j + 1)].T

    low = lax.broadcasted_iota(jnp.int32, (FR, 128), 1) < 64

    def group(s, carry):
        @pl.when(jnp.logical_or(s < 6, has13))
        def _():
            p0 = 2 * s
            wait(xbuf.at[p0], rx.at[p0])
            wait(gbuf.at[p0], rg.at[p0])

            @pl.when(s < 6)
            def _():
                wait(xbuf.at[p0 + 1], rx.at[p0 + 1])
                wait(gbuf.at[p0 + 1], rg.at[p0 + 1])

            def rows_of(i):
                return pl.ds(pl.multiple_of(i * 32, 32), 32)

            def tokens_of(i):
                return xbuf[p0 + i // 4, pl.ds((i % 4) * 4, 4)].astype(F32).reshape(32, D)

            def norm(i, carry):
                xx = tokens_of(i)
                m = jnp.mean(xx, axis=-1, keepdims=True)
                cc = xx - m
                r = lax.rsqrt(jnp.mean(cc * cc, axis=-1, keepdims=True) + EPS)
                normed[rows_of(i), :] = (cc * r * gb[0:1, :] + gb[1:2, :]).astype(BF)
                mst[rows_of(i), :] = jnp.broadcast_to(m, (32, 128))
                rst[rows_of(i), :] = jnp.broadcast_to(r, (32, 128))
                return carry

            lax.fori_loop(0, 8, norm, 0, unroll=2)

            for j in range(3):
                part = dot(normed[...], wfull[:, HD * j : HD * (j + 1)]).astype(BF)
                if j == 0:
                    part = part * jnp.asarray(0.125, BF)
                proj[:, HD * j : HD * (j + 1)] = part

            def attend(u, carry):
                rows = pl.ds(pl.multiple_of(u * FR, FR), FR)
                for h in range(3):
                    cols = slice(128 * h, 128 * (h + 1))
                    q = proj[rows, 128 * h : 128 * (h + 1)]
                    key = proj[rows, HD + 128 * h : HD + 128 * (h + 1)]
                    val = proj[rows, 2 * HD + 128 * h : 2 * HD + 128 * (h + 1)]
                    up = (gbuf[p0 + u, :, :, cols].astype(F32).reshape(FR, 128) * valid[...]).astype(BF)
                    none = jnp.zeros_like(key)
                    kk = jnp.concatenate([jnp.where(low, key, none), jnp.where(low, none, key)], axis=0)
                    vv = jnp.concatenate([jnp.where(low, val, none), jnp.where(low, none, val)], axis=0)
                    st = dot(kk, q, NT)
                    dpt = dot(vv, up, NT)
                    probs, grads = [], []
                    for half in range(2):
                        sc = st[FR * half : FR * (half + 1)] + mask[...]
                        e = jnp.exp(sc - jnp.max(sc, axis=0, keepdims=True))
                        pr = e * (1.0 / jnp.sum(e, axis=0, keepdims=True))
                        dd = dpt[FR * half : FR * (half + 1)]
                        inner = jnp.sum(pr * dd, axis=0, keepdims=True)
                        probs.append(pr.astype(BF))
                        grads.append((pr * (dd - inner)).astype(BF))
                    pb = jnp.concatenate(probs, axis=0)
                    ds = jnp.concatenate(grads, axis=0)
                    mixed = dot(pb, vv, TN) * valid[...]
                    abuf[p0 + u, :, :, cols] = mixed.reshape(16, 8, 128).astype(BF)
                    dq = dot(ds, kk, TN) * 0.125
                    dvf = dot(pb, up)
                    dkf = dot(ds, q)
                    dproj[rows, 128 * h : 128 * (h + 1)] = dq.astype(BF)
                    dproj[rows, HD + 128 * h : HD + 128 * (h + 1)] = jnp.where(low, dkf[:FR], dkf[FR:]).astype(BF)
                    dproj[rows, 2 * HD + 128 * h : 2 * HD + 128 * (h + 1)] = jnp.where(low, dvf[:FR], dvf[FR:]).astype(BF)
                return carry

            lax.fori_loop(0, 2, attend, 0)

            for j in range(3):
                ng[:, 256 * j : 256 * (j + 1)] = dot(dproj[...], wt[:, 256 * j : 256 * (j + 1)]).astype(BF)

            def back(i, carry):
                std = (tokens_of(i) - mst[rows_of(i), 0:1]) * rst[rows_of(i), 0:1]
                n = ng[rows_of(i), :].astype(F32)
                gacc[...] += jnp.sum((n * std).reshape(4, 8, D), axis=0)
                bacc[...] += jnp.sum(n.reshape(4, 8, D), axis=0)
                e = n * gb[0:1, :]
                m1 = jnp.mean(e, axis=-1, keepdims=True)
                m2 = jnp.mean(e * std, axis=-1, keepdims=True)
                tg = rst[rows_of(i), 0:1] * (e - m1 - std * m2)
                tbuf[p0 + i // 4, pl.ds((i % 4) * 4, 4)] = tg.reshape(4, 8, D).astype(BF)
                return carry

            lax.fori_loop(0, 8, back, 0, unroll=2)

            for u in range(2):
                p = p0 + u

                @pl.when(p < 13)
                def _():
                    last = p // 12
                    patch = jnp.where(p < 12, 16 * p + me, 192 + me // 5)
                    for t in tms:
                        remote(tbuf.at[p, t], tgo.at[patch], osx.at[last], orx.at[last], tm=t).start()
                        remote(abuf.at[p, t], ato.at[patch], osg.at[last], org.at[last], tm=t).start()
                    pltpu.make_async_copy(tbuf.at[p, me], tgo.at[patch], orx.at[last]).start()
                    pltpu.make_async_copy(abuf.at[p, me], ato.at[patch], org.at[last]).start()

            nt[...] = normed[...].T
            for j in range(3):
                dw[:, HD * j : HD * (j + 1)] += dot(nt[...], dproj[:, HD * j : HD * (j + 1)])

        return carry

    lax.fori_loop(0, 7, group, 0)

    def block(d):
        return dw[pl.ds(pl.multiple_of(d * 48, 8), 48), :]

    order = (4, 3, 5, 2, 6, 1, 7, 0)
    gsum = jnp.sum(gacc[...], axis=0, keepdims=True)
    bsum = jnp.sum(bacc[...], axis=0, keepdims=True)
    pk[...] = jnp.zeros_like(pk)
    for j in range(3):
        pk[j : j + 1, :] = gsum[:, 256 * j : 256 * (j + 1)]
        pk[3 + j : 4 + j, :] = bsum[:, 256 * j : 256 * (j + 1)]
    for k in order:
        senda[k] = block(zs[k] * 2 + 1 - c).astype(BF)
        remote(senda.at[k], recva.at[k], asend, arecv.at[k], dp=partner).start()
    remote(pk, pkp, k1s, k1r, dp=partner).start()
    for k in order:
        wait(recva.at[k], arecv.at[k])
        total = block(zs[k] * 2 + c) + recva[k].astype(F32)
        if k:
            sendb[k - 1] = total.astype(BF)
            remote(sendb.at[k - 1], recvb.at[k - 1], bsend, brecv.at[k - 1], dp=zs[k] * 2 + c).start()
    wait(pkp, k1r)
    pk2[...] = pk[...] + pkp[...]
    for k in range(1, 8):
        remote(pk2, pkz.at[k - 1], k2s, k2r.at[k - 1], dp=zs[k] * 2 + c).start()
    for k in (1, 7, 2, 6, 3, 5, 4):
        wait(recvb.at[k - 1], brecv.at[k - 1])
        total = total + recvb[k - 1].astype(F32)
    for j in range(9):
        totb[j] = total[:, 128 * j : 128 * (j + 1)].astype(BF)

        @pl.when(me != j)
        def _():
            remote(totb.at[j], crx.at[me], csend, crecv, tm=j).start()

        @pl.when(me == j)
        def _():
            pltpu.make_async_copy(totb.at[j], crx.at[me], crecv).start()

    packed = pk2[...]
    for k in range(1, 8):
        wait(pkz.at[k - 1], k2r.at[k - 1])
        packed = packed + pkz[k - 1]
    pk3[...] = packed
    for t in tms:
        remote(pk3, pkt.at[me], k3s, k3r, tm=t).start()
    pltpu.make_async_copy(pk3, pkt.at[me], k3r).start()

    @pl.when(me < 9)
    def _():
        wait(crx, crecv)
        red[...] = jnp.sum(crx[...].astype(F32), axis=0).astype(BF)
        for t in tms:
            remote(red, fin.at[me], fsend, frecv, tm=t).start()
        pltpu.make_async_copy(red, fin.at[me], frecv).start()

    wait(pkt, k3r)
    gbo[...] = jnp.sum(pkt[...], axis=0)
    wait(fin, frecv)
    for j in range(9):
        dwo[:, 128 * j : 128 * (j + 1)] = fin[j].astype(F32)

    wait(tgo.at[pl.ds(0, 192)], orx.at[0])
    wait(ato.at[pl.ds(0, 192)], org.at[0])
    wait(tgo.at[pl.ds(192, 4)], orx.at[1])
    wait(ato.at[pl.ds(192, 4)], org.at[1])
    wait(tgo.at[pl.ds(0, 180)], osx.at[0])
    wait(ato.at[pl.ds(0, 180)], osg.at[0])

    @pl.when(has13)
    def _():
        wait(tgo.at[pl.ds(0, 15)], osx.at[1])
        wait(ato.at[pl.ds(0, 15)], osg.at[1])
        wait(xt.at[pl.ds(0, 183)], sx)
        wait(gt.at[pl.ds(0, 183)], sg)

    @pl.when(jnp.logical_not(has13))
    def _():
        wait(xt.at[pl.ds(0, 184)], sx)
        wait(gt.at[pl.ds(0, 184)], sg)

    wait(wall.at[pl.ds(0, 7)], wsend)
    wait(wall.at[pl.ds(0, 8)], psend)
    wait(senda, asend)
    wait(sendb, bsend)
    wait(pk, k1s)
    wait(pkz, k2s)
    wait(pkt.at[pl.ds(0, 15)], k3s)

    @pl.when(me < 9)
    def _():
        wait(totb.at[pl.ds(0, 8)], csend)
        wait(crx.at[pl.ds(0, 15)], fsend)

    @pl.when(me >= 9)
    def _():
        wait(totb, csend)


def masks(frame_count, starts, kept):
    index = jnp.arange(FR, dtype=jnp.int32)
    clip = jnp.zeros((FR,), jnp.int32)
    for b in range(1, starts.shape[0]):
        clip = clip + jnp.where(index >= b * BLOCK, starts[b], 0)
    usable = (index < frame_count) & (kept == 1)
    allowed = (clip[:, None] == clip[None, :]) & (usable[:, None] | (index[:, None] == index[None, :]))
    valid = jnp.broadcast_to((index < frame_count)[:, None], (FR, 128))
    return jnp.where(allowed, 0.0, MASKED).astype(F32), jnp.where(valid, 1.0, 0.0).astype(F32)


def body(video_tokens, norm_gain, norm_bias, qkv_weight, frame_counts, clip_starts, frame_kept, attended_grad):
    dp = lax.axis_index("dp")
    xt = video_tokens[0].transpose(1, 0, 2)
    gt = attended_grad[0].transpose(1, 0, 2)
    mask, valid = masks(frame_counts[0], clip_starts[0], frame_kept[0])
    rows = jnp.zeros((8, C), BF)
    rows = lax.dynamic_update_slice(rows, jnp.stack([norm_gain, norm_bias]), (0, dp * 48))
    wl = jnp.concatenate([qkv_weight, rows], axis=0)
    vmem = pltpu.VMEM
    sems = pltpu.SemaphoreType.DMA
    any_spec = pl.BlockSpec(memory_space=pl.ANY)
    vspec = pl.BlockSpec(memory_space=pltpu.VMEM)
    ato, tgo, dwo, gbo = pl.pallas_call(
        kernel,
        out_shape=(
            jax.ShapeDtypeStruct((196, 8, HD), BF),
            jax.ShapeDtypeStruct((196, 8, D), BF),
            jax.ShapeDtypeStruct((48, C), F32),
            jax.ShapeDtypeStruct((8, 256), F32),
        ),
        in_specs=[any_spec, any_spec, any_spec, vspec, vspec],
        out_specs=(any_spec, any_spec, vspec, vspec),
        scratch_shapes=[
            vmem((14, 16, 8, D), BF), vmem((14, 16, 8, HD), BF),
            vmem((14, 16, 8, HD), BF), vmem((14, 16, 8, D), BF),
            vmem((16, WB, C), BF), vmem((D, C), BF), vmem((C, D), BF), vmem((D, C), F32), vmem((8, D), F32),
            vmem((256, D), BF), vmem((256, 128), F32), vmem((256, 128), F32),
            vmem((256, C), BF), vmem((256, C), BF), vmem((D, 256), BF), vmem((256, D), BF),
            vmem((8, D), F32), vmem((8, D), F32),
            vmem((8, 48, C), BF), vmem((8, 48, C), BF), vmem((7, 48, C), BF), vmem((7, 48, C), BF),
            vmem((9, 48, 128), BF), vmem((16, 48, 128), BF), vmem((48, 128), BF), vmem((9, 48, 128), BF),
            vmem((8, 256), F32), vmem((8, 256), F32), vmem((8, 256), F32), vmem((7, 8, 256), F32),
            vmem((8, 256), F32), vmem((16, 8, 256), F32),
            sems((13,)), sems((13,)), sems, sems, sems((2,)), sems((2,)), sems((2,)), sems((2,)),
            sems, sems((8,)), sems, sems, sems,
            sems, sems((8,)), sems, sems((7,)), sems, sems, sems, sems,
            sems, sems, sems, sems((7,)), sems, sems,
        ],
        compiler_params=pltpu.CompilerParams(
            collective_id=0, has_side_effects=True, vmem_limit_bytes=58 * 2**20
        ),
    )(xt, gt, wl, mask, valid)
    attended = ato.transpose(1, 0, 2)[None]
    tokens_grad = tgo.transpose(1, 0, 2)[None]
    flat = gbo.reshape(2048)
    gain = lax.dynamic_slice(flat, (dp * 48,), (48,))
    bias = lax.dynamic_slice(flat, (D + dp * 48,), (48,))
    return attended, tokens_grad, dwo, gain, bias


def solution(mesh):
    placed = (
        P("dp", "tm", None, None), P("dp"), P("dp"), P("dp", None),
        P("dp"), P("dp", None), P("dp", None), P("dp", "tm", None, None),
    )
    return jax.shard_map(
        body,
        mesh=mesh,
        in_specs=placed,
        out_specs=(P("dp", "tm", None, None), P("dp", "tm", None, None), P("dp", None), P("dp"), P("dp")),
        check_vma=False,
    )
```
